32 devices in a mesh: qa: 4 (over z), qb: 8 (over y, x, core).
Axes of the slice: x: 2, y: 2, z: 4, core: 2. Of those that a mesh axis runs over, the one named last changes fastest.
Arguments:
- state: float32 [4, 8, 32, 128, 128], P('qa', 'qb'), may hold values from -6 to 6
- angles: float32 [2, 24], replicated, may hold values from -3.140625 to 3.140625
- order: int32 [2, 34], replicated, may hold values from 0 to 33, each once within a row
- fixed_bits: int32 [10], replicated, may hold values 0 or 1
Outputs:
- evolved: float32 [4, 8, 32, 128, 128], P('qa', 'qb')
The draws below stay inside these ranges and needn't reach their ends.
Inputs may be any that keep to these rules, and one draw needn't show every extreme that they name: `order`: each row is a permutation of the 34 labels; labels under 24 are window qubits, the others name entries of fixed_bits.
All inputs are finite; a program needn't handle non-finite values.
Results may differ from the reference program's by a relative error of at most 0.0003.
Values sent between devices are 32-bit elements; how exact they have to be, the bound alone decides.
No kernel may reach another device: no remote copies, remote signals or barrier semaphores. Data moves between devices by JAX's collectives and lax.ppermute only.
A program may use at most 128 MiB of HBM per device.

```python
import jax
import jax.numpy as jnp
from jax import lax

LAYERS = 2
GATE_QUBITS = 7
FIXED_QUBITS = 10
GATE = 128
BLOCKS = 32
GLOBAL_QUBITS = 5
WINDOW_QUBITS = 24
LABELS = 34
N_QA = 4
N_QB = 8


def plant(drawn, own_key, smallest, largest):
    dims = drawn.shape
    spot = [jax.random.randint(jax.random.fold_in(own_key, axis), (), 0, dims[axis]) for axis in range(len(dims))]
    drawn = drawn.at[tuple(spot)].set(smallest)
    longest = dims.index(max(dims))
    spot[longest] = (spot[longest] + 1) % dims[longest]
    return drawn.at[tuple(spot)].set(largest)


def block_levels(own_key, shape, split, smallest, largest):
    factor_of, own = 1.0, jax.random.fold_in(own_key, 6)
    for position, parts in split:
        draws = jnp.exp(jax.random.uniform(jax.random.fold_in(own, position), (parts,), jnp.float32, smallest / len(split), largest / len(split)))
        factor_of = factor_of * jnp.repeat(draws, shape[position] // parts).reshape([-1 if axis == position else 1 for axis in range(len(shape))])
    return factor_of


def gaussian(key, shape, scale, reach, pieces=(), kind=jnp.bfloat16):
    factor_of = block_levels(key, shape, pieces, -0.22, 0.18) if pieces else 1.0
    result = jax.random.normal(key, shape, jnp.float32) * scale * factor_of
    return jnp.minimum(jnp.maximum(result, -reach), reach).astype(kind)


def setup_inputs(seed: int = 0) -> dict:
    key_of = jax.random.split(jax.random.key(seed), 5)
    state = gaussian(key_of[0], (N_QA, N_QB, BLOCKS, GATE, GATE), 1.0, 6.0, ((0, 4), (1, 8)), jnp.float32)
    angles = jnp.clip(jax.random.uniform(key_of[1], (LAYERS, WINDOW_QUBITS), jnp.float32, -3.140625, 3.140625), -3.140625, 3.140625)
    order = jax.vmap(lambda own: jax.random.permutation(own, LABELS))(jax.random.split(key_of[2], LAYERS)).reshape((LAYERS, LABELS)).astype(jnp.int32)
    fixed_bits = plant((jax.random.randint(key_of[3], (FIXED_QUBITS,), 0, 2) < 1).astype(jnp.int32), jax.random.fold_in(key_of[3], 1), 0, 1)
    return {"state": state, "angles": angles, "order": order, "fixed_bits": fixed_bits}


def joined_gate(block_angles):
    count = block_angles.shape[0]
    order_size = 2 ** count
    out_rows = jnp.arange(order_size, dtype=jnp.int32)[:, None]
    in_columns = jnp.arange(order_size, dtype=jnp.int32)[None, :]
    cosine = jnp.cos(block_angles / 2.0)
    sine = jnp.sin(block_angles / 2.0)
    product = jnp.ones((order_size, order_size), jnp.float32)
    for bit_index in range(count):
        out_bit = jnp.bitwise_and(jnp.right_shift(out_rows, bit_index), 1)
        in_bit = jnp.bitwise_and(jnp.right_shift(in_columns, bit_index), 1)
        entry = jnp.where(out_bit == in_bit, cosine[bit_index], jnp.where(out_bit == 1, sine[bit_index], -sine[bit_index]))
        product = product * entry
    return product


def apply_middle(gate_matrix, three_dims):
    return jnp.einsum('oi,aib->aob', gate_matrix, three_dims, precision=lax.Precision.HIGHEST)


def qubit_bits(labels, extent, offset, count):
    positions = jnp.arange(extent, dtype=jnp.int32)
    shifts = labels - offset
    inside = (shifts >= 0) & (shifts < count)
    clipped = jnp.clip(shifts, 0, count - 1)
    bits = jnp.bitwise_and(jnp.right_shift(positions[None, :], clipped[:, None]), 1)
    return jnp.where(inside[:, None], bits, 0).astype(jnp.float32)


def fixed_value(labels, fixed_bits, window):
    slots = jnp.arange(fixed_bits.shape[0], dtype=jnp.int32)
    hits = (labels[:, None] - window) == slots[None, :]
    return jnp.sum(jnp.where(hits, fixed_bits[None, :], 0), axis=1).astype(jnp.float32)


def sign_tables(order_row, parity_offset, fixed_bits, gate_qubits, global_qubits):
    gate_order = 2 ** gate_qubits
    blocks = 2 ** global_qubits
    window = 2 * gate_qubits + 2 * global_qubits
    layout = [(blocks, 2 * gate_qubits + global_qubits, global_qubits), (blocks, 2 * gate_qubits, global_qubits), (gate_order, gate_qubits, gate_qubits), (gate_order, 0, gate_qubits)]
    pair_count = (order_row.shape[0] - parity_offset) // 2
    first = order_row[parity_offset:parity_offset + 2 * pair_count:2]
    second = order_row[parity_offset + 1:parity_offset + 2 * pair_count:2]
    first_bits = [qubit_bits(first, extent, offset, count) for extent, offset, count in layout]
    second_bits = [qubit_bits(second, extent, offset, count) for extent, offset, count in layout]
    first_fixed = fixed_value(first, fixed_bits, window)
    second_fixed = fixed_value(second, fixed_bits, window)
    constant = jnp.sum(first_fixed * second_fixed)
    singles = [jnp.sum(first_bits[dim_index] * second_bits[dim_index] + second_fixed[:, None] * first_bits[dim_index] + first_fixed[:, None] * second_bits[dim_index], axis=0) for dim_index in range(4)]
    cross_tables = {}
    for left_dim in range(4):
        for right_dim in range(left_dim + 1, 4):
            forward = jnp.einsum('pi,pj->ij', first_bits[left_dim], second_bits[right_dim], precision=lax.Precision.HIGHEST)
            backward = jnp.einsum('pi,pj->ji', first_bits[right_dim], second_bits[left_dim], precision=lax.Precision.HIGHEST)
            cross_tables[(left_dim, right_dim)] = forward + backward
    return constant, singles, cross_tables


def parity_signs(tables, local_is_device, remote_index):
    constant, singles, cross_tables = tables
    if local_is_device:
        local_dim, remote_dim = 0, 1
        local_remote = cross_tables[(0, 1)]
    else:
        local_dim, remote_dim = 1, 0
        local_remote = jnp.transpose(cross_tables[(0, 1)])

    def pick_row(table):
        return lax.dynamic_index_in_dim(table, remote_index, 0, keepdims=False)

    column = lax.dynamic_index_in_dim(local_remote, remote_index, 1, keepdims=False)
    parity_sum = constant + pick_row(singles[remote_dim])
    parity_sum = parity_sum + (singles[local_dim] + column)[:, None, None]
    parity_sum = parity_sum + (singles[2] + pick_row(cross_tables[(remote_dim, 2)]))[None, :, None]
    parity_sum = parity_sum + (singles[3] + pick_row(cross_tables[(remote_dim, 3)]))[None, None, :]
    parity_sum = parity_sum + cross_tables[(local_dim, 2)][:, :, None] + cross_tables[(local_dim, 3)][:, None, :]
    parity_sum = parity_sum + cross_tables[(2, 3)][None, :, :]
    odd = jnp.bitwise_and(parity_sum.astype(jnp.int32), 1)
    return (1 - 2 * odd).astype(jnp.float32)


def reference(state, angles, order, fixed_bits):
    amplitudes = state.reshape(BLOCKS, BLOCKS, GATE, GATE)
    for layer_index in range(LAYERS):
        row_angles = angles[layer_index]
        low_gate = joined_gate(row_angles[0:GATE_QUBITS])
        high_gate = joined_gate(row_angles[GATE_QUBITS:2 * GATE_QUBITS])
        top_gate = joined_gate(row_angles[2 * GATE_QUBITS:2 * GATE_QUBITS + GLOBAL_QUBITS])
        device_gate = joined_gate(row_angles[2 * GATE_QUBITS + GLOBAL_QUBITS:WINDOW_QUBITS])
        amplitudes = jnp.dot(amplitudes.reshape(-1, GATE), jnp.transpose(low_gate), precision=lax.Precision.HIGHEST)
        amplitudes = apply_middle(high_gate, amplitudes.reshape(BLOCKS * BLOCKS, GATE, GATE))
        amplitudes = apply_middle(top_gate, amplitudes.reshape(BLOCKS, BLOCKS, GATE * GATE))
        amplitudes = jnp.dot(device_gate, amplitudes.reshape(BLOCKS, -1), precision=lax.Precision.HIGHEST)
        tables = sign_tables(order[layer_index], layer_index % 2, fixed_bits, GATE_QUBITS, GLOBAL_QUBITS)

        def flip(inputs):
            slab, device_row = inputs
            return slab * parity_signs(tables, False, device_row)

        amplitudes = lax.map(flip, (amplitudes.reshape(BLOCKS, BLOCKS, GATE, GATE), jnp.arange(BLOCKS, dtype=jnp.int32)))
    return amplitudes.reshape(state.shape)
```

```python
import functools

import jax
import jax.numpy as jnp
from jax import lax
from jax.experimental import pallas as pl
from jax.experimental.pallas import tpu as pltpu
from jax.sharding import PartitionSpec as P

LANES = 128
SUB = 8
AXES = ("qa", "qb")


def bit_groups(count):
    if count <= 5:
        return [tuple(range(count))]
    half = (count + 1) // 2
    return [tuple(range(half)), tuple(range(half, count))]


def rotate_values(values, pairs):
    for bit, (cosine, sine) in enumerate(pairs):
        step = 1 << bit
        new = list(values)
        for index in range(len(values)):
            if index & step == 0:
                first, second = values[index], values[index + step]
                new[index] = cosine * first - sine * second
                new[index + step] = sine * first + cosine * second
        values = new
    return values


def gate_matrix(cs_ref, layer, first, count, transpose):
    order = 1 << count
    rows = lax.broadcasted_iota(jnp.int32, (order, order), 0)
    cols = lax.broadcasted_iota(jnp.int32, (order, order), 1)
    out, inn = (cols, rows) if transpose else (rows, cols)
    product = jnp.ones((order, order), jnp.float32)
    for bit in range(count):
        cosine = cs_ref[layer, 0, first + bit]
        sine = cs_ref[layer, 1, first + bit]
        out_bit = jnp.bitwise_and(jnp.right_shift(out, bit), 1)
        in_bit = jnp.bitwise_and(jnp.right_shift(inn, bit), 1)
        entry = jnp.where(out_bit == in_bit, cosine, jnp.where(out_bit == 1, sine, -sine))
        product = product * entry
    return product


def split(value):
    high = value.astype(jnp.bfloat16)
    low = (value - high.astype(jnp.float32)).astype(jnp.bfloat16)
    return high, low


def local_kernel(layer, with_sign, cs_ref, x_ref, *rest):
    if with_sign:
        sign_ref, out_ref, mid, low_gate, high_gate = rest
    else:
        out_ref, mid, low_gate, high_gate = rest
    blocks, order, _ = x_ref.shape
    gate_qubits = order.bit_length() - 1
    block_qubits = blocks.bit_length() - 1
    zero = jnp.zeros((order, order), jnp.bfloat16)
    gh, gl = split(gate_matrix(cs_ref, layer, 0, gate_qubits, True))
    low_gate[:order, :order] = gh
    low_gate[:order, order:] = gl
    low_gate[order:, :order] = gh
    low_gate[order:, order:] = zero
    gh, gl = split(gate_matrix(cs_ref, layer, gate_qubits, gate_qubits, False))
    high_gate[:order, :order] = gh
    high_gate[order:, :order] = gl
    high_gate[:order, order:] = gh
    high_gate[order:, order:] = zero

    def two_blocks(pair, carry):
        rows = x_ref[pl.ds(2 * pair, 2)].reshape(2 * order, order)
        high, low = split(rows)
        both = jnp.dot(
            jnp.concatenate([high, low], axis=1),
            low_gate[...],
            preferred_element_type=jnp.float32,
        )
        rows = both[:, :order] + both[:, order:]
        side = jnp.concatenate([rows[:order], rows[order:]], axis=1)
        high, low = split(side)
        both = jnp.dot(
            high_gate[...],
            jnp.concatenate([high, low], axis=0),
            preferred_element_type=jnp.float32,
        )
        side = both[:order] + both[order:]
        mid[2 * pair] = side[:, :order]
        mid[2 * pair + 1] = side[:, order:]
        return carry

    lax.fori_loop(0, blocks // 2, two_blocks, 0)

    groups = bit_groups(block_qubits)
    for number, bits in enumerate(groups):
        last = number == len(groups) - 1
        width = 1 << len(bits)
        stride = 1 << bits[0]
        pairs = [
            (cs_ref[layer, 0, 2 * gate_qubits + bit], cs_ref[layer, 1, 2 * gate_qubits + bit])
            for bit in bits
        ]

        def tile(index, carry):
            start = pl.multiple_of(lax.rem(index, order // SUB) * SUB, SUB)
            base = index // (order // SUB)
            if stride == 1:
                base = base * width
            where = [base + step * stride for step in range(width)]
            values = [mid[spot, pl.ds(start, SUB), :] for spot in where]
            values = rotate_values(values, pairs)
            for spot, value in zip(where, values):
                if last and with_sign:
                    value = value * sign_ref[spot, pl.ds(start, SUB), :]
                if last:
                    out_ref[spot, pl.ds(start, SUB), :] = value
                else:
                    mid[spot, pl.ds(start, SUB), :] = value
            return carry

        lax.fori_loop(0, (blocks // width) * (order // SUB), tile, 0)


def local_rotate(layer, cs, x, sign):
    blocks, order, _ = x.shape
    args = (cs, x) if sign is None else (cs, x, sign)
    vmem = pl.BlockSpec(memory_space=pltpu.VMEM)
    return pl.pallas_call(
        functools.partial(local_kernel, layer, sign is not None),
        out_shape=jax.ShapeDtypeStruct(x.shape, x.dtype),
        in_specs=[pl.BlockSpec(memory_space=pltpu.SMEM)] + [vmem] * (len(args) - 1),
        out_specs=vmem,
        scratch_shapes=[
            pltpu.VMEM(x.shape, jnp.float32),
            pltpu.VMEM((2 * order, 2 * order), jnp.bfloat16),
            pltpu.VMEM((2 * order, 2 * order), jnp.bfloat16),
        ],
        cost_estimate=pl.CostEstimate(
            flops=12 * x.size * order, bytes_accessed=8 * x.size, transcendentals=0
        ),
        name=f"local_{layer}",
    )(*args)


def global_kernel(first_qubit, cs_ref, x_ref, sign_ref, out_ref):
    blocks, rows, _ = x_ref.shape
    count = blocks.bit_length() - 1
    groups = bit_groups(count)
    passes = [(0, bits) for bits in groups] + [(1, bits) for bits in groups]
    source = x_ref
    if len(groups) == 1:
        plan = [passes]
    else:
        plan = [[entry] for entry in passes]
    for number, entries in enumerate(plan):
        bits = entries[0][1]
        width = 1 << len(bits)
        stride = 1 << bits[0]
        signed = len(groups) == 1 or number == len(groups)

        def tile(index, carry, entries=entries, source=source, signed=signed):
            start = pl.multiple_of(lax.rem(index, rows // SUB) * SUB, SUB)
            base = index // (rows // SUB)
            if stride == 1:
                base = base * width
            where = [base + step * stride for step in range(width)]
            values = [source[spot, pl.ds(start, SUB), :] for spot in where]
            for layer, own_bits in entries:
                if layer == 1 and signed:
                    values = [
                        value * sign_ref[spot, pl.ds(start, SUB), :]
                        for spot, value in zip(where, values)
                    ]
                pairs = [
                    (cs_ref[layer, 0, first_qubit + bit], cs_ref[layer, 1, first_qubit + bit])
                    for bit in own_bits
                ]
                values = rotate_values(values, pairs)
            for spot, value in zip(where, values):
                out_ref[spot, pl.ds(start, SUB), :] = value
            return carry

        lax.fori_loop(0, (blocks // width) * (rows // SUB), tile, 0)
        source = out_ref


def global_rotate(cs, x, sign, first_qubit):
    blocks, order, lanes = x.shape
    rows = order // 4
    block = pl.BlockSpec((blocks, rows, lanes), lambda i: (0, i, 0))
    return pl.pallas_call(
        functools.partial(global_kernel, first_qubit),
        grid=(order // rows,),
        out_shape=jax.ShapeDtypeStruct(x.shape, x.dtype),
        in_specs=[pl.BlockSpec(memory_space=pltpu.SMEM), block, block],
        out_specs=block,
        cost_estimate=pl.CostEstimate(
            flops=40 * x.size, bytes_accessed=12 * x.size, transcendentals=0
        ),
        name="global_01",
    )(cs, x, sign)


def sign_kernel(parity_offset, window, swapped, order_ref, fixed_ref, place_ref, out_ref):
    blocks, rows, lanes = out_ref.shape
    low_bits = (rows * lanes).bit_length() - 1
    block_bits = blocks.bit_length() - 1
    pairs = (order_ref.shape[0] - parity_offset) // 2
    place = place_ref[0]
    spots = (
        lax.broadcasted_iota(jnp.int32, (rows, lanes), 0) * lanes
        + lax.broadcasted_iota(jnp.int32, (rows, lanes), 1)
    )

    def label_terms(label):
        inside = label < window
        shift = jnp.where(inside, label, 0)
        keep = jnp.where(inside, 1, 0)
        slot = jnp.clip(label - window, 0, fixed_ref.shape[0] - 1)
        return shift, keep, jnp.where(inside, 0, fixed_ref[slot])

    terms = []
    for k in range(pairs):
        terms.append(
            label_terms(order_ref[parity_offset + 2 * k])
            + label_terms(order_ref[parity_offset + 2 * k + 1])
        )

    def one_block(block, carry):
        if swapped:
            upper = block * blocks + place
        else:
            upper = place * blocks + block
        index = spots + (upper << low_bits)
        total = jnp.zeros((rows, lanes), jnp.int32)
        for s1, k1, f1, s2, k2, f2 in terms:
            first = ((index >> s1) & k1) | f1
            second = ((index >> s2) & k2) | f2
            total = total ^ (first & second)
        out_ref[block] = (1 - 2 * total).astype(jnp.float32)
        return carry

    lax.fori_loop(0, blocks, one_block, 0)


def make_sign(order_row, fixed_bits, place, parity_offset, window, swapped, shape):
    smem = pl.BlockSpec(memory_space=pltpu.SMEM)
    return pl.pallas_call(
        functools.partial(sign_kernel, parity_offset, window, swapped),
        out_shape=jax.ShapeDtypeStruct(shape, jnp.float32),
        in_specs=[smem, smem, smem],
        out_specs=pl.BlockSpec(memory_space=pltpu.VMEM),
        name=f"sign_{parity_offset}",
    )(order_row, fixed_bits, place)


def body(state, angles, order, fixed_bits):
    blocks, gate_order, lanes = state.shape[2:]
    low_qubits = 2 * (gate_order.bit_length() - 1)
    block_qubits = blocks.bit_length() - 1
    window = angles.shape[1]
    half = angles / 2.0
    cs = jnp.stack([jnp.cos(half), jnp.sin(half)], axis=1)
    place = (lax.axis_index("qa") * lax.axis_size("qb") + lax.axis_index("qb")).reshape(1)
    x = state.reshape(blocks, gate_order, lanes)

    def exchange(value):
        return lax.all_to_all(value, AXES, split_axis=0, concat_axis=0, tiled=True)

    x = local_rotate(0, cs, x, None)
    x = exchange(x)
    sign = make_sign(order[0], fixed_bits, place, 0, window, True, x.shape)
    x = global_rotate(cs, x, sign, low_qubits + block_qubits)
    x = exchange(x)
    sign = make_sign(order[1], fixed_bits, place, 1, window, False, x.shape)
    x = local_rotate(1, cs, x, sign)
    return x.reshape(state.shape)


def solution(mesh):
    in_specs = (P("qa", "qb", None, None, None), P(), P(), P())
    out_specs = P("qa", "qb", None, None, None)
    return jax.shard_map(body, mesh=mesh, in_specs=in_specs, out_specs=out_specs, check_vma=False)
```
